128 devices in a mesh: chan: 32 (over y_hi, x, z), win: 4 (over y_lo, core).
Axes of the slice: x: 4, y: 4 (y_hi: 2, y_lo: 2; y = y_hi * 2 + y_lo), z: 4, core: 2. Of those that a mesh axis runs over, the one named last changes fastest.
Arguments:
- records: bfloat16 [10240, 102400], P('chan', 'win'), may hold values from -6 to 6
- offsets: int32 [32], P('win'), may hold values from 0 to 128
- src_index: int32 [4, 4], replicated, may hold values from 0 to 10239, as said below
- quality: int32 [10240], P('chan'), may hold values 0 or 1
Outputs:
- stacks: float32 [4, 196, 10240], P('win', None, 'chan')
The draws below stay inside these ranges and needn't reach their ends.
Inputs may be any that keep to these rules, and one draw needn't show every extreme that they name: `src_index`: the 4 channels of one step are distinct and lie in one aligned block of 320 channels; some step includes channel 0 and some other step the last channel.
All inputs are finite; a program needn't handle non-finite values. No bound on the sum of `quality` on one device may be relied on, other than what follows from the above.
Results may differ from the reference program's by a relative error of at most 0.0038.
Values may be sent and summed in bfloat16 or wider, within the bound.
A program may use at most 256 MiB of HBM per device.

```python
import math
import jax
import jax.numpy as jnp
from jax import lax

C = 10240
L = 3072
LAGS = 49
NSRC = 4
STEPS = 4
GAP = 128
STRIDE = 3200
SEGMENTS = 32
SAMPLES = 102400
CH_DEV = 320


def draw_src_index(key, part):
    key_owner = jax.random.fold_in(key, 11)
    key_local = jax.random.fold_in(key, 12)
    key_pick = jax.random.fold_in(key, 13)
    key_other = jax.random.fold_in(key, 14)
    key_high = jax.random.fold_in(key, 15)
    key_low = jax.random.fold_in(key, 16)
    owner = jax.random.randint(key_owner, (STEPS, 1), 0, C // CH_DEV)
    chosen = jnp.stack([jax.random.permutation(jax.random.fold_in(key_local, number), CH_DEV)[:NSRC] for number in range(STEPS)])
    high_row = jnp.concatenate([jax.random.permutation(key_high, CH_DEV - 1)[:NSRC - 1], jnp.full((1,), CH_DEV - 1, jnp.int32)])
    low_row = jnp.concatenate([jnp.zeros((1,), jnp.int32), 1 + jax.random.permutation(key_low, CH_DEV - 1)[:NSRC - 1]])
    first = jax.random.randint(key_pick, (), 0, STEPS)
    second = (first + 1 + jax.random.randint(key_other, (), 0, STEPS - 1)) % STEPS
    rows = jnp.arange(STEPS, dtype=jnp.int32)[:, None]
    chosen = jnp.where(rows == first, high_row[None, :], jnp.where(rows == second, low_row[None, :], chosen))
    owner = jnp.where(rows == first, C // CH_DEV - 1, jnp.where(rows == second, 0, owner))
    return (owner * CH_DEV + chosen).astype(jnp.int32)


def draw_offsets(key, part):
    key_value = jax.random.fold_in(key, 21)
    key_first = jax.random.fold_in(key, 22)
    key_second = jax.random.fold_in(key, 23)
    values = jax.random.randint(key_value, (SEGMENTS,), 0, GAP + 1)
    first = jax.random.randint(key_first, (), 0, SEGMENTS)
    second = (first + 1 + jax.random.randint(key_second, (), 0, SEGMENTS - 1)) % SEGMENTS
    values = values.at[first].set(GAP).at[second].set(0)
    return values.astype(jnp.int32)


def touch_ends(values, stream_key, least, largest):
    place = [jax.random.randint(jax.random.fold_in(stream_key, axis), (), 0, length) for axis, length in enumerate(values.shape)]
    widest = values.shape.index(max(values.shape))
    neighbour = place[:widest] + [(place[widest] + 1) % values.shape[widest]] + place[widest + 1:]
    return values.at[tuple(place)].set(least).at[tuple(neighbour)].set(largest)


def levels(rng, dims, split, low, largest):
    gain, own = 1.0, jax.random.fold_in(rng, 6)
    for axis_at, shards_of in split:
        draws = jnp.exp(jax.random.uniform(jax.random.fold_in(own, axis_at), (shards_of,), jnp.float32, low / len(split), largest / len(split)))
        gain = gain * jnp.repeat(draws, dims[axis_at] // shards_of).reshape([-1 if axis == axis_at else 1 for axis in range(len(dims))])
    return gain


def bell_draw(stream_key, shape, width, reach, split=(), kind=jnp.bfloat16):
    array = jax.random.normal(stream_key, shape, jnp.float32) * width
    if len(split) > 0:
        array = levels(stream_key, shape, split, -0.22, 0.18) * array
    return jnp.clip(array, min=-reach, max=reach).astype(kind)


def setup_inputs(seed: int = 0) -> dict:
    splits = jax.random.split(jax.random.key(seed), 5)
    return {
        "records": bell_draw(splits[0], (C, SAMPLES), 1.0, 6.0, ((0, 32), (1, 4))),
        "offsets": draw_offsets(jax.random.fold_in(splits[4], 71), 0),
        "src_index": draw_src_index(jax.random.fold_in(splits[4], 71), 0),
        "quality": touch_ends((jax.random.randint(splits[3], (C,), 0, 8) < 7).astype(jnp.int32), jax.random.fold_in(splits[3], 1), 0, 1),
    }


EPSILON = 1e-06

def whiten(segment):
    values = segment.astype(jnp.float32)
    power = lax.optimization_barrier(jnp.mean(values * values, axis=-1, keepdims=True))
    return (values / jnp.sqrt(power + EPSILON)).astype(jnp.bfloat16)

def lagged(source):
    half = (LAGS - 1) // 2
    length = source.shape[-1]
    widths = [(0, 0)] * (source.ndim - 1) + [(half, half)]
    padded = jnp.pad(source, widths)
    return jnp.stack([padded[..., 2 * half - column:2 * half - column + length] for column in range(LAGS)], axis=-2)

def reference(records, offsets, src_index, quality):
    starts = jnp.arange(SEGMENTS, dtype=jnp.int32) * STRIDE + offsets.astype(jnp.int32)

    def accumulate(total, begin):
        segment = lax.dynamic_slice_in_dim(records, begin, L, 1)
        white = whiten(segment)
        sources = white[src_index]
        shifted = lagged(sources).reshape(STEPS, NSRC * LAGS, L)
        term = jnp.einsum('kpt,ct->kpc', shifted.astype(jnp.float32), white.astype(jnp.float32), precision=lax.Precision.HIGHEST)
        return (total + term, None)
    initial = jnp.zeros((STEPS, NSRC * LAGS, C), jnp.float32)
    total, _ = lax.scan(accumulate, initial, starts)
    scale = 1.0 / math.sqrt(SEGMENTS * L)
    return total * scale * quality.astype(jnp.float32)[None, None, :]
```

```python
import functools
import math

import jax
import jax.numpy as jnp
from jax import lax
from jax.experimental import pallas as pl
from jax.experimental.pallas import tpu as pltpu
from jax.sharding import PartitionSpec as P

L = 3072
LAGS = 49
EPSILON = 1e-06
LANES = 128
PIECE = 256
EIGHT = 8
PAD = 64
MESH = pl.DeviceIdType.MESH
VMEM_BYTES = 60 << 20


class Sizes:
    def __init__(self, channels, samples, segs, steps, srcs, chans, wins):
        self.channels, self.segs, self.steps, self.srcs = channels, segs, steps, srcs
        self.chans, self.wins = chans, wins
        self.width = samples // segs
        self.tiles = self.width // LANES
        self.rows = steps * srcs
        self.piece_tiles = PIECE // LANES
        self.pieces = -(-self.tiles // self.piece_tiles)
        self.plane = chans // 2
        self.side = math.isqrt(self.plane)
        self.groups = -(-LAGS // EIGHT)
        self.zrows = self.width + 2 * PAD
        assert self.rows * EIGHT == LANES and self.side**2 == self.plane and wins == 4
        assert self.pieces == self.plane - self.side + 1


def in_segment(z, tile, value, off):
    if 0 < tile < z.tiles - 1:
        return value
    lane = lax.broadcasted_iota(jnp.int32, value.shape, 1)
    return jnp.where(lane >= off if tile == 0 else lane < off, value, 0.0)


def pick(z, records, seg, onehot, off, cand):
    rows = jnp.dot(onehot, records[seg], preferred_element_type=jnp.float32)
    tiles = [in_segment(z, t, rows[:, t * LANES : (t + 1) * LANES], off) for t in range(z.tiles)]
    power = jnp.sum(sum(value * value for value in tiles), axis=1, keepdims=True) * (1.0 / L)
    factor = 1.0 / jnp.sqrt(power + EPSILON)
    for t, value in enumerate(tiles):
        lanes = t % z.piece_tiles * LANES
        cand[seg, t // z.piece_tiles, :, lanes : lanes + LANES] = (value * factor).astype(jnp.bfloat16)
    for t in range(z.tiles, z.pieces * z.piece_tiles):
        lanes = t % z.piece_tiles * LANES
        cand[seg, t // z.piece_tiles, :, lanes : lanes + LANES] = jnp.zeros((z.rows, LANES), jnp.bfloat16)


def measure_power(z, records, seg, off, factors):
    count = 32

    @pl.loop(0, z.channels // count)
    def _(block):
        at = pl.ds(pl.multiple_of(block * count, count), count)
        total = jnp.zeros((count, LANES), jnp.float32)
        for t in range(z.tiles):
            value = in_segment(z, t, records[seg, at, t * LANES : (t + 1) * LANES].astype(jnp.float32), off)
            if t == 0 or t == z.tiles - 1:
                records[seg, at, t * LANES : (t + 1) * LANES] = value.astype(jnp.bfloat16)
            total = total + value * value
        power = jnp.sum(total, axis=1, keepdims=True) * (1.0 / L)
        factors[seg, at, :] = jnp.broadcast_to(1.0 / jnp.sqrt(power + EPSILON), (count, LANES))


def spread_lags(z, full, seg, turned):
    lane = lax.broadcasted_iota(jnp.int32, (z.rows, LANES), 1)
    zero = jnp.zeros((z.rows, LANES), jnp.bfloat16)

    def tile(t):
        if t < 0 or t >= z.tiles:
            return zero
        lanes = t % z.piece_tiles * LANES
        return full[seg, t // z.piece_tiles, :, lanes : lanes + LANES]

    before = [zero] * EIGHT
    turned[0:PAD, :] = jnp.zeros((PAD, LANES), jnp.bfloat16)
    for t in range(z.tiles + 1):
        now = tile(t)
        rolled = [now] + [pltpu.roll(now, e, 1) if t < z.tiles else zero for e in range(1, EIGHT)]
        stack = [now] + [jnp.where(lane < e, before[e], rolled[e]) for e in range(1, EIGHT)]
        block = jnp.concatenate(stack, axis=0).T
        if t < z.tiles:
            turned[PAD + t * LANES : PAD + (t + 1) * LANES, :] = block
        else:
            turned[PAD + z.width : z.zrows, :] = block[0:PAD]
        before = rolled


def correlate(z, records, seg, factors, turned, total):
    half = z.groups // 2
    for first in range(0, z.groups, 2):
        groups = range(first, min(first + 2, z.groups))
        lagged = jnp.concatenate(
            [turned[PAD - EIGHT * (a - half) : PAD - EIGHT * (a - half) + z.width, :] for a in groups], axis=1
        )
        term = lax.dot_general(records[seg], lagged, (((1,), (0,)), ((), ())), preferred_element_type=jnp.float32)
        for n, a in enumerate(groups):
            scaled = term[:, n * LANES : (n + 1) * LANES] * factors[seg]
            at = slice(a * LANES, (a + 1) * LANES)
            total[:, at] = scaled if seg == 0 else total[:, at] + scaled


def service_order(z):
    tasks, done = [], 0.0
    for seg in range(z.segs):
        at = 3.0 + 1.5 * seg
        late = (("choose", 0.0), ("power", 1.0), ("first", 3.3), ("second", 6.1), ("publish", 9.0), ("forward", 11.8))
        tasks += [(at + lag, seg, name) for name, lag in late]
        done = max(at + 15.0, done + 2.7)
        tasks.append((done, seg, "product"))
    return [(name, seg) for _, seg, name in sorted(tasks)]


def main_kernel(
    z, src_index, offsets, records_hbm, out,
    records, factors, cand, recv_first, part, recv_second, mine, other, full, turned_a, turned_b, total, flipped,
    blocks, pair_in, near_out, near_in,
    load_sem, first_send, first_recv, second_send, second_recv, y_send, y_recv, near_send, near_recv, group_send,
    group_recv, win_send, win_recv,
):
    chan, win = lax.axis_index("chan"), lax.axis_index("win")
    plane, place = chan // z.plane * z.plane, chan % z.plane
    across = (chan + z.plane) % z.chans
    core_peer = win + 1 - 2 * (win % 2)
    y_peer = (win + 2) % 4
    diagonal = (core_peer + 2) % 4
    side = z.side
    coords = (place // side, place % side)
    strides = (side, 1)
    whole_groups = z.pieces // side

    def peer(axis, step):
        at = coords[axis]
        return chan + ((at + step) % side - at) * strides[axis]

    def group_at(seg, step=0):
        return (coords[seg % 2] + step + seg // 2) % side

    def sub_at(seg, step=0):
        return (coords[1 - seg % 2] + step + seg) % side

    def is_piece(seg, step=0):
        return (group_at(seg) < whole_groups) | (sub_at(seg, step) == 0)

    def load(seg):
        return pltpu.make_async_copy(
            records_hbm.at[:, pl.ds(seg * z.width, z.width)], records.at[seg], load_sem.at[seg]
        )

    for seg in range(z.segs):
        load(seg).start()

    barrier = pltpu.get_barrier_semaphore()
    for axis in range(2):
        for step in range(1, side):
            pl.semaphore_signal(barrier, inc=1, device_id={"chan": peer(axis, step)}, device_id_type=MESH)
    pl.semaphore_signal(barrier, inc=1, device_id={"chan": across}, device_id_type=MESH)
    pl.semaphore_signal(barrier, inc=1, device_id={"win": core_peer}, device_id_type=MESH)
    pl.semaphore_signal(barrier, inc=1, device_id={"win": y_peer}, device_id_type=MESH)
    peers = 2 * (side - 1) + 3

    def remote(src, dst, send, recv, chan_to):
        return pltpu.make_async_remote_copy(
            src_ref=src, dst_ref=dst, send_sem=send, recv_sem=recv, device_id={"chan": chan_to}, device_id_type=MESH
        )

    steps = range(1, side)

    def to_group(seg, step):
        group, axis = group_at(seg, step), seg % 2
        send, recv = first_send.at[seg, step - 1], first_recv.at[seg, step - 1]
        whole = remote(
            cand.at[seg, pl.ds(group * side, side)], recv_first.at[seg, step - 1], send, recv, peer(axis, step)
        )
        single = remote(
            cand.at[seg, pl.ds(group * side, 1)], recv_first.at[seg, step - 1, pl.ds(0, 1)], send, recv,
            peer(axis, step),
        )
        return group < whole_groups, whole, single

    def to_piece(seg, step):
        copy = remote(
            part.at[seg, sub_at(seg, step)], recv_second.at[seg, step - 1], second_send.at[seg, step - 1],
            second_recv.at[seg, step - 1], peer(1 - seg % 2, step),
        )
        return is_piece(seg, step), copy

    def exchange(seg):
        return remote(mine.at[seg, 0], other.at[seg], y_send.at[seg], y_recv.at[seg], across)

    def piece_here(seg):
        return group_at(seg) * side + sub_at(seg)

    def to_line(seg, step):
        return remote(
            mine.at[seg, 1], full.at[seg, piece_here(seg)], near_send.at[seg, step - 1], near_recv.at[seg, step - 1],
            peer(1 - seg % 2, step),
        )

    def to_all(seg, step):
        send, recv, to = group_send.at[seg, step - 1], group_recv.at[seg, step - 1], peer(seg % 2, step)
        whole = full.at[seg, pl.ds(group_at(seg) * side, side)]
        single = full.at[seg, pl.ds(group_at(seg) * side, 1)]
        return remote(whole, whole, send, recv, to), remote(single, single, send, recv, to)

    def either(test, yes, no):
        pl.when(test)(yes)
        pl.when(jnp.logical_not(test))(no)

    def offer(seg):
        for step in steps:
            test, whole, single = to_group(seg, step)
            either(test, whole.start, single.start)

    def first(seg):
        def sum_pieces(count):
            for step in steps:
                to_group(seg, step)[1 if count > 1 else 2].wait_recv()
            for n in range(count):
                value = cand[seg, group_at(seg) * side + n]
                for step in steps:
                    value = value + recv_first[seg, step - 1, n]
                part[seg, n] = value

        either(group_at(seg) < whole_groups, lambda: sum_pieces(side), lambda: sum_pieces(1))
        for step in steps:
            test, copy = to_piece(seg, step)
            pl.when(test)(copy.start)

    def second(seg):
        @pl.when(is_piece(seg))
        def _():
            for step in steps:
                to_piece(seg, step)[1].wait_recv()
            value = part[seg, sub_at(seg)]
            for step in steps:
                value = value + recv_second[seg, step - 1]
            mine[seg, 0] = value
            exchange(seg).start()

    def publish(seg):
        @pl.when(is_piece(seg))
        def _():
            exchange(seg).wait_recv()
            value = mine[seg, 0] + other[seg]
            mine[seg, 1] = value
            for step in steps:
                to_line(seg, step).start()
            full[seg, piece_here(seg)] = value

    def forward(seg):
        for step in steps:
            pl.when(is_piece(seg, side - step))(to_line(seg, step).wait_recv)
        for step in steps:
            whole, single = to_all(seg, step)
            either(group_at(seg) < whole_groups, whole.start, single.start)

    def arrive(seg):
        for step in steps:
            whole, single = to_all(seg, step)
            either(group_at(seg, side - step) < whole_groups, whole.wait_recv, single.wait_recv)

    def drain(seg):
        for step in steps:
            test, whole, single = to_group(seg, step)
            either(test, whole.wait_send, single.wait_send)
            test, copy = to_piece(seg, step)
            pl.when(test)(copy.wait_send)
            whole, single = to_all(seg, step)
            either(group_at(seg) < whole_groups, whole.wait_send, single.wait_send)

        @pl.when(is_piece(seg))
        def _():
            exchange(seg).wait_send()
            for step in steps:
                to_line(seg, step).wait_send()

    row = lax.broadcasted_iota(jnp.int32, (z.rows, z.channels), 0)
    wanted_row = jnp.zeros((z.rows, z.channels), jnp.int32)
    for n in range(z.rows):
        wanted_row = jnp.where(row == n, src_index[n // z.srcs, n % z.srcs], wanted_row)
    held = lax.broadcasted_iota(jnp.int32, (z.rows, z.channels), 1) + chan * z.channels
    onehot = (held == wanted_row).astype(jnp.float32).astype(jnp.bfloat16)

    def choose(seg):
        load(seg).wait()
        pick(z, records, seg, onehot, offsets[seg], cand)

    def power(seg):
        measure_power(z, records, seg, offsets[seg], factors)

    turned = (turned_a, turned_b)

    def product(seg):
        arrive(seg)
        spread_lags(z, full, seg, turned[seg % 2])
        correlate(z, records, seg, factors, turned[seg % 2], total)

    tasks = {
        "power": power, "first": first, "second": second, "publish": publish, "forward": forward, "product": product,
    }
    for name, seg in service_order(z):
        if name == "choose":
            choose(seg)
            if seg == 0:
                pl.semaphore_wait(barrier, peers)
            offer(seg)
        else:
            tasks[name](seg)

    for at in range(0, z.channels, LANES):
        count = min(LANES, z.channels - at)
        flipped[at // LANES, :, 0:count] = total[at : at + count, :].T
        for step in range(z.steps):
            for i in range(z.srcs):
                value = flipped[at // LANES, pl.ds(step * z.srcs + i, LAGS, stride=z.rows), :]
                blocks[step, i * LAGS : (i + 1) * LAGS, at : at + count] = value[:, 0:count]

    def send(src, dst, number, peer):
        return pltpu.make_async_remote_copy(
            src_ref=src, dst_ref=dst, send_sem=win_send.at[number], recv_sem=win_recv.at[number],
            device_id={"win": peer}, device_id_type=MESH,
        )

    length = z.srcs * LAGS
    cut = length // 4 // EIGHT * EIGHT
    parts = [pl.ds(n * cut, cut if n < 3 else length - 3 * cut) for n in range(4)]
    far = [send(blocks.at[diagonal, at], pair_in.at[1, at], n, core_peer) for n, at in enumerate(parts)]
    own = [send(blocks.at[core_peer, at], pair_in.at[0, at], 4 + n, core_peer) for n, at in enumerate(parts)]
    last = [send(near_out.at[at], near_in.at[at], 8 + n, y_peer) for n, at in enumerate(parts)]
    for copy in far + own:
        copy.start()
    for n, at in enumerate(parts):
        far[n].wait_recv()
        near_out[at] = blocks[y_peer, at] + pair_in[1, at]
        last[n].start()
    for n, at in enumerate(parts):
        own[n].wait_recv()
        last[n].wait_recv()
        out[0, at] = blocks[win, at] + pair_in[0, at] + near_in[at]

    for seg in range(z.segs):
        drain(seg)
    for copy in far + own + last:
        copy.wait_send()


def body(chans, wins, records, offsets, src_index, quality):
    z = Sizes(*records.shape, offsets.shape[0], *src_index.shape, chans, wins)
    smem = pl.BlockSpec(memory_space=pltpu.SMEM)
    vmem = pl.BlockSpec(memory_space=pltpu.VMEM)
    hbm = pl.BlockSpec(memory_space=pl.ANY)
    bf16, f32 = jnp.bfloat16, jnp.float32
    dma = pltpu.SemaphoreType.DMA
    piece = (z.rows, PIECE)
    block = (z.srcs * LAGS, z.channels)
    sums = pl.pallas_call(
        functools.partial(main_kernel, z),
        out_shape=jax.ShapeDtypeStruct((1, *block), f32),
        in_specs=[smem, smem, hbm],
        out_specs=vmem,
        scratch_shapes=[
            pltpu.VMEM((z.segs, z.channels, z.width), bf16),
            pltpu.VMEM((z.segs, z.channels, LANES), f32),
            pltpu.VMEM((z.segs, z.plane, *piece), bf16),
            pltpu.VMEM((z.segs, z.side - 1, z.side, *piece), bf16),
            pltpu.VMEM((z.segs, z.side, *piece), bf16),
            pltpu.VMEM((z.segs, z.side - 1, *piece), bf16),
            pltpu.VMEM((z.segs, 2, *piece), bf16),
            pltpu.VMEM((z.segs, *piece), bf16),
            pltpu.VMEM((z.segs, z.plane, *piece), bf16),
            pltpu.VMEM((z.zrows, LANES), bf16),
            pltpu.VMEM((z.zrows, LANES), bf16),
            pltpu.VMEM((z.channels, z.groups * LANES), f32),
            pltpu.VMEM((-(-z.channels // LANES), z.groups * LANES, LANES), f32),
            pltpu.VMEM((z.steps, *block), f32),
            pltpu.VMEM((2, *block), f32),
            pltpu.VMEM(block, f32),
            pltpu.VMEM(block, f32),
            dma((z.segs,)),
            dma((z.segs, z.side - 1)),
            dma((z.segs, z.side - 1)),
            dma((z.segs, z.side - 1)),
            dma((z.segs, z.side - 1)),
            dma((z.segs,)),
            dma((z.segs,)),
            dma((z.segs, z.side - 1)),
            dma((z.segs, z.side - 1)),
            dma((z.segs, z.side - 1)),
            dma((z.segs, z.side - 1)),
            dma((12,)),
            dma((12,)),
        ],
        compiler_params=pltpu.CompilerParams(
            collective_id=0, has_side_effects=True, vmem_limit_bytes=VMEM_BYTES
        ),
        name="stack",
    )(src_index, offsets, records)
    scale = 1.0 / math.sqrt(z.segs * z.wins * L)
    return sums * scale * quality.astype(f32)[None, None, :]


def solution(mesh):
    return jax.shard_map(
        functools.partial(body, mesh.shape["chan"], mesh.shape["win"]),
        mesh=mesh,
        in_specs=(P("chan", "win"), P("win"), P(), P("chan")),
        out_specs=P("win", None, "chan"),
        check_vma=False,
    )
```

```python
import functools
import math

import jax
import jax.numpy as jnp
from jax import lax
from jax.experimental import pallas as pl
from jax.experimental.pallas import tpu as pltpu
from jax.sharding import PartitionSpec as P

L = 3072
LAGS = 49
EPSILON = 1e-06
LANES = 128
FIRST_PART = 192
EIGHT = 8
PAD = 64
MESH = pl.DeviceIdType.MESH
VMEM_BYTES = 60 << 20


class Sizes:
    def __init__(self, channels, samples, segs, steps, srcs, chans, wins):
        self.channels, self.segs, self.steps, self.srcs = channels, segs, steps, srcs
        self.chans, self.wins = chans, wins
        self.width = samples // segs
        self.tiles = self.width // LANES
        self.rows = steps * srcs
        self.plane = chans // 2
        self.side = math.isqrt(self.plane)
        self.pair = 2 * self.side
        self.slots = self.side * self.pair
        self.whole_groups = self.tiles // self.pair
        self.groups = -(-LAGS // EIGHT)
        self.zrows = self.width + 2 * PAD
        assert self.rows * EIGHT == LANES and self.side**2 == self.plane and wins == 4
        assert self.tiles == self.whole_groups * self.pair + 1 and self.whole_groups == self.side - 1


def in_segment(z, tile, value, off):
    if 0 < tile < z.tiles - 1:
        return value
    lane = lax.broadcasted_iota(jnp.int32, value.shape, 1)
    return jnp.where(lane >= off if tile == 0 else lane < off, value, 0.0)


def pick(z, records, seg, onehot, off, cand):
    rows = jnp.dot(onehot, records[seg], preferred_element_type=jnp.float32)
    tiles = [in_segment(z, t, rows[:, t * LANES : (t + 1) * LANES], off) for t in range(z.tiles)]
    power = jnp.sum(sum(value * value for value in tiles), axis=1, keepdims=True) * (1.0 / L)
    factor = 1.0 / jnp.sqrt(power + EPSILON)
    for t, value in enumerate(tiles):
        cand[seg, t] = (value * factor).astype(jnp.bfloat16)


def measure_power(z, records, seg, off, factors):
    count = 32

    @pl.loop(0, z.channels // count)
    def _(block):
        at = pl.ds(pl.multiple_of(block * count, count), count)
        total = jnp.zeros((count, LANES), jnp.float32)
        for t in range(z.tiles):
            value = in_segment(z, t, records[seg, at, t * LANES : (t + 1) * LANES].astype(jnp.float32), off)
            if t == 0 or t == z.tiles - 1:
                records[seg, at, t * LANES : (t + 1) * LANES] = value.astype(jnp.bfloat16)
            total = total + value * value
        power = jnp.sum(total, axis=1, keepdims=True) * (1.0 / L)
        factors[seg, at, :] = jnp.broadcast_to(1.0 / jnp.sqrt(power + EPSILON), (count, LANES))


def spread_lags(z, full, seg, turned):
    lane = lax.broadcasted_iota(jnp.int32, (z.rows, LANES), 1)
    zero = jnp.zeros((z.rows, LANES), jnp.bfloat16)

    def tile(t):
        return full[seg, t] if t < z.tiles else zero

    before = [zero] * EIGHT
    turned[seg, 0:PAD, :] = jnp.zeros((PAD, LANES), jnp.bfloat16)
    for t in range(z.tiles + 1):
        now = tile(t)
        rolled = [now] + [pltpu.roll(now, e, 1) if t < z.tiles else zero for e in range(1, EIGHT)]
        stack = [now] + [jnp.where(lane < e, before[e], rolled[e]) for e in range(1, EIGHT)]
        block = jnp.concatenate(stack, axis=0).T
        if t < z.tiles:
            turned[seg, PAD + t * LANES : PAD + (t + 1) * LANES, :] = block
        else:
            turned[seg, PAD + z.width : z.zrows, :] = block[0:PAD]
        before = rolled


def correlate(z, records, seg, rows, factors, turned, total):
    half = z.groups // 2
    for first in range(0, z.groups, 2):
        groups = range(first, min(first + 2, z.groups))
        starts = [PAD - EIGHT * (a - half) for a in groups]
        lagged = jnp.concatenate([turned[seg, at : at + z.width, :] for at in starts], axis=1)
        term = jnp.dot(records[seg, rows, :], lagged, preferred_element_type=jnp.float32)
        for n, a in enumerate(groups):
            scaled = term[:, n * LANES : (n + 1) * LANES] * factors[seg, rows, :]
            at = slice(a * LANES, (a + 1) * LANES)
            total[rows, at] = scaled if seg == 0 else total[rows, at] + scaled


def service_order(z):
    tasks, done = [], 0.0
    for seg in range(z.segs):
        at = 3.0 + 1.3 * seg
        late = (("choose", 0.0), ("power", 1.5), ("first", 4.3), ("second", 8.4), ("forward", 12.5))
        tasks += [(at + lag, seg, name) for name, lag in late]
        done = max(at + 16.6, done + 1.5)
        tasks.append((done, seg, "product"))
    return [(name, seg) for _, seg, name in sorted(tasks)]


def main_kernel(
    z, src_index, offsets, records_hbm, out,
    records, factors, cand, recv_first, part, recv_second, mine, full, turned, total, flipped,
    blocks_a, pair_a, near_out_a, near_in_a, blocks_b, pair_b, near_out_b, near_in_b,
    load_sem, first_send, first_recv, second_send, second_recv, line_send, line_recv, group_send, group_recv,
    win_send, win_recv,
):
    chan, win = lax.axis_index("chan"), lax.axis_index("win")
    place = chan % z.plane
    level = chan // z.plane
    core_peer = win + 1 - 2 * (win % 2)
    y_peer = (win + 2) % 4
    diagonal = (core_peer + 2) % 4
    side = z.side
    coords = (place // side, place % side)
    strides = (side, 1)
    whole_groups = z.whole_groups

    def peer(axis, step, up=0):
        at = coords[axis]
        return (chan + ((at + step) % side - at) * strides[axis] + up * z.plane) % z.chans

    def group_at(seg, step=0):
        return (coords[seg % 2] + step + seg // 2) % side

    def slot_at(seg, step=0, up=0):
        return (coords[1 - seg % 2] + step + seg) % side * 2 + (level + up) % 2

    def kept(seg, step=0, up=0):
        return (group_at(seg) < whole_groups) | (slot_at(seg, step, up) == 0)

    def load(seg):
        return pltpu.make_async_copy(
            records_hbm.at[:, pl.ds(seg * z.width, z.width)], records.at[seg], load_sem.at[seg]
        )

    for seg in range(z.segs):
        load(seg).start()

    barrier = pltpu.get_barrier_semaphore()
    for axis in range(2):
        for step in range(1, side):
            pl.semaphore_signal(barrier, inc=1, device_id={"chan": peer(axis, step)}, device_id_type=MESH)
            pl.semaphore_signal(barrier, inc=1, device_id={"chan": peer(axis, step, 1)}, device_id_type=MESH)
    pl.semaphore_signal(barrier, inc=1, device_id={"chan": peer(0, 0, 1)}, device_id_type=MESH)
    pl.semaphore_signal(barrier, inc=1, device_id={"win": core_peer}, device_id_type=MESH)
    pl.semaphore_signal(barrier, inc=1, device_id={"win": y_peer}, device_id_type=MESH)
    peers = 4 * (side - 1) + 3

    def remote(src, dst, send, recv, chan_to):
        return pltpu.make_async_remote_copy(
            src_ref=src, dst_ref=dst, send_sem=send, recv_sem=recv, device_id={"chan": chan_to}, device_id_type=MESH
        )

    steps = range(1, side)
    moves = [(step, up) for step in range(side) for up in range(2)][1:]

    def to_group(seg, step):
        group, to = group_at(seg, step), peer(seg % 2, step)
        send, recv = first_send.at[seg, step - 1], first_recv.at[seg, step - 1]
        whole = remote(cand.at[seg, pl.ds(group * z.pair, z.pair)], recv_first.at[seg, step - 1], send, recv, to)
        single = remote(
            cand.at[seg, pl.ds(group * z.pair, 1)], recv_first.at[seg, step - 1, pl.ds(0, 1)], send, recv, to
        )
        return group < whole_groups, whole, single

    def to_slot(seg, n):
        step, up = moves[n]
        return kept(seg, step, up), remote(
            part.at[seg, slot_at(seg, step, up)], recv_second.at[seg, n], second_send.at[seg, n],
            second_recv.at[seg, n], peer(1 - seg % 2, step, up),
        )

    def tile_here(seg):
        return group_at(seg) * z.pair + slot_at(seg)

    def to_line(seg, n):
        return remote(
            mine.at[seg], full.at[seg, tile_here(seg)], line_send.at[seg, n], line_recv.at[seg, n],
            peer(1 - seg % 2, *moves[n]),
        )

    def to_all(seg, step):
        send, recv, to = group_send.at[seg, step - 1], group_recv.at[seg, step - 1], peer(seg % 2, step)
        whole = full.at[seg, pl.ds(group_at(seg) * z.pair, z.pair)]
        single = full.at[seg, pl.ds(group_at(seg) * z.pair, 1)]
        return remote(whole, whole, send, recv, to), remote(single, single, send, recv, to)

    def either(test, yes, no):
        pl.when(test)(yes)
        pl.when(jnp.logical_not(test))(no)

    def offer(seg):
        for step in steps:
            test, whole, single = to_group(seg, step)
            either(test, whole.start, single.start)

    def first(seg):
        def sum_tiles(count):
            for step in steps:
                to_group(seg, step)[1 if count > 1 else 2].wait_recv()
            for n in range(count):
                value = cand[seg, group_at(seg) * z.pair + n]
                for step in steps:
                    value = value + recv_first[seg, step - 1, n]
                part[seg, n] = value

        either(group_at(seg) < whole_groups, lambda: sum_tiles(z.pair), lambda: sum_tiles(1))
        for n in range(len(moves)):
            test, copy = to_slot(seg, n)
            pl.when(test)(copy.start)

    def second(seg):
        @pl.when(kept(seg))
        def _():
            for n in range(len(moves)):
                to_slot(seg, n)[1].wait_recv()
            value = part[seg, slot_at(seg)]
            for n in range(len(moves)):
                value = value + recv_second[seg, n]
            mine[seg] = value
            for n in range(len(moves)):
                to_line(seg, n).start()
            full[seg, tile_here(seg)] = value

    def forward(seg):
        for n, (step, up) in enumerate(moves):
            pl.when(kept(seg, side - step, up))(to_line(seg, n).wait_recv)
        for step in steps:
            whole, single = to_all(seg, step)
            either(group_at(seg) < whole_groups, whole.start, single.start)

    def arrive(seg):
        for step in steps:
            whole, single = to_all(seg, step)
            either(group_at(seg, side - step) < whole_groups, whole.wait_recv, single.wait_recv)

    def drain(seg):
        for step in steps:
            test, whole, single = to_group(seg, step)
            either(test, whole.wait_send, single.wait_send)
            whole, single = to_all(seg, step)
            either(group_at(seg) < whole_groups, whole.wait_send, single.wait_send)
        for n in range(len(moves)):
            test, copy = to_slot(seg, n)
            pl.when(test)(copy.wait_send)

        @pl.when(kept(seg))
        def _():
            for n in range(len(moves)):
                to_line(seg, n).wait_send()

    row = lax.broadcasted_iota(jnp.int32, (z.rows, z.channels), 0)
    wanted_row = jnp.zeros((z.rows, z.channels), jnp.int32)
    for n in range(z.rows):
        wanted_row = jnp.where(row == n, src_index[n // z.srcs, n % z.srcs], wanted_row)
    held = lax.broadcasted_iota(jnp.int32, (z.rows, z.channels), 1) + chan * z.channels
    onehot = (held == wanted_row).astype(jnp.float32).astype(jnp.bfloat16)

    def choose(seg):
        load(seg).wait()
        pick(z, records, seg, onehot, offsets[seg], cand)

    def power(seg):
        measure_power(z, records, seg, offsets[seg], factors)

    rows_a, rows_b = slice(0, FIRST_PART), slice(FIRST_PART, z.channels)

    def product(seg):
        arrive(seg)
        spread_lags(z, full, seg, turned)
        correlate(z, records, seg, rows_a, factors, turned, total)

    tasks = {"power": power, "first": first, "second": second, "forward": forward, "product": product}
    for name, seg in service_order(z):
        if name == "choose":
            choose(seg)
            if seg == 0:
                pl.semaphore_wait(barrier, peers)
            offer(seg)
        else:
            tasks[name](seg)

    def flip(rows, blocks):
        for at in range(rows.start, rows.stop, LANES):
            count, to = min(LANES, rows.stop - at), at - rows.start
            flipped[:, 0:count] = total[at : at + count, :].T
            for step in range(z.steps):
                for i in range(z.srcs):
                    value = flipped[pl.ds(step * z.srcs + i, LAGS, stride=z.rows), :]
                    blocks[step, i * LAGS : (i + 1) * LAGS, to : to + count] = value[:, 0:count]

    def send(src, dst, number, to):
        return pltpu.make_async_remote_copy(
            src_ref=src, dst_ref=dst, send_sem=win_send.at[number], recv_sem=win_recv.at[number],
            device_id={"win": to}, device_id_type=MESH,
        )

    def sum_over_win(number, blocks, pair_in, near_out, near_in):
        far = send(blocks.at[diagonal], pair_in.at[1], number, core_peer)
        own = send(blocks.at[core_peer], pair_in.at[0], number + 1, core_peer)
        last = send(near_out, near_in, number + 2, y_peer)

        def begin():
            far.start()
            own.start()

        def turn():
            far.wait_recv()
            near_out[...] = blocks[y_peer] + pair_in[1]
            last.start()

        def end():
            own.wait_recv()
            last.wait_recv()
            return blocks[win] + pair_in[0] + near_in[...]

        return begin, turn, end, (far, own, last)

    begin_a, turn_a, end_a, copies_a = sum_over_win(0, blocks_a, pair_a, near_out_a, near_in_a)
    begin_b, turn_b, end_b, copies_b = sum_over_win(3, blocks_b, pair_b, near_out_b, near_in_b)
    flip(rows_a, blocks_a)
    begin_a()
    for seg in range(z.segs):
        if seg == z.segs // 2:
            turn_a()
        correlate(z, records, seg, rows_b, factors, turned, total)
    flip(rows_b, blocks_b)
    begin_b()
    for seg in range(z.segs):
        drain(seg)
    out[0, :, rows_a] = end_a()
    turn_b()
    out[0, :, rows_b] = end_b()
    for copy in copies_a + copies_b:
        copy.wait_send()


def body(chans, wins, records, offsets, src_index, quality):
    z = Sizes(*records.shape, offsets.shape[0], *src_index.shape, chans, wins)
    smem = pl.BlockSpec(memory_space=pltpu.SMEM)
    vmem = pl.BlockSpec(memory_space=pltpu.VMEM)
    hbm = pl.BlockSpec(memory_space=pl.ANY)
    bf16, f32 = jnp.bfloat16, jnp.float32
    dma = pltpu.SemaphoreType.DMA
    tile = (z.rows, LANES)
    block = (z.srcs * LAGS, z.channels)
    moves = 2 * z.side - 1
    shares = []
    for width in (FIRST_PART, z.channels - FIRST_PART):
        share = (block[0], width)
        shares += [pltpu.VMEM(lead + share, f32) for lead in ((z.steps,), (2,), (), ())]
    sums = pl.pallas_call(
        functools.partial(main_kernel, z),
        out_shape=jax.ShapeDtypeStruct((1, *block), f32),
        in_specs=[smem, smem, hbm],
        out_specs=vmem,
        scratch_shapes=[
            pltpu.VMEM((z.segs, z.channels, z.width), bf16),
            pltpu.VMEM((z.segs, z.channels, LANES), f32),
            pltpu.VMEM((z.segs, z.slots, *tile), bf16),
            pltpu.VMEM((z.segs, z.side - 1, z.pair, *tile), bf16),
            pltpu.VMEM((z.segs, z.pair, *tile), bf16),
            pltpu.VMEM((z.segs, moves, *tile), bf16),
            pltpu.VMEM((z.segs, *tile), bf16),
            pltpu.VMEM((z.segs, z.slots, *tile), bf16),
            pltpu.VMEM((z.segs, z.zrows, LANES), bf16),
            pltpu.VMEM((z.channels, z.groups * LANES), f32),
            pltpu.VMEM((z.groups * LANES, LANES), f32),
            *shares,
            dma((z.segs,)),
            dma((z.segs, z.side - 1)),
            dma((z.segs, z.side - 1)),
            dma((z.segs, moves)),
            dma((z.segs, moves)),
            dma((z.segs, moves)),
            dma((z.segs, moves)),
            dma((z.segs, z.side - 1)),
            dma((z.segs, z.side - 1)),
            dma((6,)),
            dma((6,)),
        ],
        compiler_params=pltpu.CompilerParams(
            collective_id=0, has_side_effects=True, vmem_limit_bytes=VMEM_BYTES
        ),
        name="stack",
    )(src_index, offsets, records)
    scale = 1.0 / math.sqrt(z.segs * z.wins * L)
    return sums * scale * quality.astype(f32)[None, None, :]


def solution(mesh):
    return jax.shard_map(
        functools.partial(body, mesh.shape["chan"], mesh.shape["win"]),
        mesh=mesh,
        in_specs=(P("chan", "win"), P("win"), P(), P("chan")),
        out_specs=P("win", None, "chan"),
        check_vma=False,
    )
```

```python
import functools
import math

import jax
import jax.numpy as jnp
from jax import lax
from jax.experimental import pallas as pl
from jax.experimental.pallas import tpu as pltpu
from jax.sharding import PartitionSpec as P

L = 3072
LAGS = 49
EPSILON = 1e-06
LANES = 128
FIRST_PART = 192
EIGHT = 8
PAD = 64
MESH = pl.DeviceIdType.MESH
VMEM_BYTES = 60 << 20


class Sizes:
    def __init__(self, channels, samples, segs, steps, srcs, chans, wins):
        self.channels, self.segs, self.steps, self.srcs = channels, segs, steps, srcs
        self.chans, self.wins = chans, wins
        self.width = samples // segs
        self.tiles = self.width // LANES
        self.rows = steps * srcs
        self.plane = chans // 2
        self.side = math.isqrt(self.plane)
        self.pair = 2 * self.side
        self.slots = self.side * self.pair
        self.whole_groups = self.tiles // self.pair
        self.groups = -(-LAGS // EIGHT)
        self.zrows = self.width + 2 * PAD
        assert self.rows * EIGHT == LANES and self.side**2 == self.plane and wins == 4
        assert self.tiles == self.whole_groups * self.pair + 1 and self.whole_groups == self.side - 1


def in_segment(z, tile, value, off):
    if 0 < tile < z.tiles - 1:
        return value
    lane = lax.broadcasted_iota(jnp.int32, value.shape, 1)
    return jnp.where(lane >= off if tile == 0 else lane < off, value, 0.0)


def pick(z, records, seg, onehot, off, cand):
    rows = jnp.dot(onehot, records[seg], preferred_element_type=jnp.float32)
    tiles = [in_segment(z, t, rows[:, t * LANES : (t + 1) * LANES], off) for t in range(z.tiles)]
    power = jnp.sum(sum(value * value for value in tiles), axis=1, keepdims=True) * (1.0 / L)
    factor = 1.0 / jnp.sqrt(power + EPSILON)
    for t, value in enumerate(tiles):
        cand[seg, t] = (value * factor).astype(jnp.bfloat16)


def measure_power(z, records, seg, off, factors):
    count = 32

    @pl.loop(0, z.channels // count)
    def _(block):
        at = pl.ds(pl.multiple_of(block * count, count), count)
        total = jnp.zeros((count, LANES), jnp.float32)
        for t in range(z.tiles):
            value = in_segment(z, t, records[seg, at, t * LANES : (t + 1) * LANES].astype(jnp.float32), off)
            if t == 0 or t == z.tiles - 1:
                records[seg, at, t * LANES : (t + 1) * LANES] = value.astype(jnp.bfloat16)
            total = total + value * value
        power = jnp.sum(total, axis=1, keepdims=True) * (1.0 / L)
        factors[seg, at, :] = jnp.broadcast_to(1.0 / jnp.sqrt(power + EPSILON), (count, LANES))


def spread_lags(z, full, seg, turned):
    lane = lax.broadcasted_iota(jnp.int32, (z.rows, LANES), 1)
    zero = jnp.zeros((z.rows, LANES), jnp.bfloat16)

    def tile(t):
        return full[seg, t] if t < z.tiles else zero

    before = [zero] * EIGHT
    turned[seg, 0:PAD, :] = jnp.zeros((PAD, LANES), jnp.bfloat16)
    for t in range(z.tiles + 1):
        now = tile(t)
        rolled = [now] + [pltpu.roll(now, e, 1) if t < z.tiles else zero for e in range(1, EIGHT)]
        stack = [now] + [jnp.where(lane < e, before[e], rolled[e]) for e in range(1, EIGHT)]
        block = jnp.concatenate(stack, axis=0).T
        if t < z.tiles:
            turned[seg, PAD + t * LANES : PAD + (t + 1) * LANES, :] = block
        else:
            turned[seg, PAD + z.width : z.zrows, :] = block[0:PAD]
        before = rolled


def correlate(z, records, seg, rows, factors, turned, total):
    half = z.groups // 2
    for first in range(0, z.groups, 2):
        groups = range(first, min(first + 2, z.groups))
        starts = [PAD - EIGHT * (a - half) for a in groups]
        lagged = jnp.concatenate([turned[seg, at : at + z.width, :] for at in starts], axis=1)
        term = jnp.dot(records[seg, rows, :], lagged, preferred_element_type=jnp.float32)
        for n, a in enumerate(groups):
            scaled = term[:, n * LANES : (n + 1) * LANES] * factors[seg, rows, :]
            at = slice(a * LANES, (a + 1) * LANES)
            total[rows, at] = scaled if seg == 0 else total[rows, at] + scaled


def service_order(z):
    tasks, done = [], 0.0
    for seg in range(z.segs):
        at = 3.0 + 1.3 * seg
        late = (("choose", 0.0), ("power", 2.5), ("first", 5.0), ("second", 10.2), ("forward", 15.4))
        tasks += [(at + lag, seg, name) for name, lag in late]
        done = max(at + 20.4, done + 1.5)
        tasks.append((done, seg, "product"))
    return [(name, seg) for _, seg, name in sorted(tasks)]


def main_kernel(
    z, src_index, offsets, records_hbm, out,
    records, factors, cand, recv_first, part, recv_second, mine, full, turned, total, flipped,
    blocks_a, pair_a, near_out_a, near_in_a, blocks_b, pair_b, near_out_b, near_in_b,
    load_sem, first_send, first_recv, second_send, second_recv, line_send, line_recv, group_send, group_recv,
    win_send, win_recv,
):
    chan, win = lax.axis_index("chan"), lax.axis_index("win")
    place = chan % z.plane
    level = chan // z.plane
    core_peer = win + 1 - 2 * (win % 2)
    y_peer = (win + 2) % 4
    diagonal = (core_peer + 2) % 4
    side = z.side
    coords = (place // side, place % side)
    strides = (side, 1)
    whole_groups = z.whole_groups

    def peer(axis, step, up=0):
        at = coords[axis]
        return (chan + ((at + step) % side - at) * strides[axis] + up * z.plane) % z.chans

    def group_at(seg, step=0):
        return (coords[seg % 2] + step + seg // 2) % side

    def slot_at(seg, step=0, up=0):
        return (coords[1 - seg % 2] + step + seg) % side * 2 + (level + up) % 2

    def kept(seg, step=0, up=0):
        return (group_at(seg) < whole_groups) | (slot_at(seg, step, up) == 0)

    def load(seg):
        return pltpu.make_async_copy(
            records_hbm.at[:, pl.ds(seg * z.width, z.width)], records.at[seg], load_sem.at[seg]
        )

    for seg in range(z.segs):
        load(seg).start()

    barrier = pltpu.get_barrier_semaphore()
    for axis in range(2):
        for step in range(1, side):
            pl.semaphore_signal(barrier, inc=1, device_id={"chan": peer(axis, step)}, device_id_type=MESH)
            pl.semaphore_signal(barrier, inc=1, device_id={"chan": peer(axis, step, 1)}, device_id_type=MESH)
    pl.semaphore_signal(barrier, inc=1, device_id={"chan": peer(0, 0, 1)}, device_id_type=MESH)
    pl.semaphore_signal(barrier, inc=1, device_id={"win": core_peer}, device_id_type=MESH)
    pl.semaphore_signal(barrier, inc=1, device_id={"win": y_peer}, device_id_type=MESH)
    peers = 4 * (side - 1) + 3

    def remote(src, dst, send, recv, chan_to):
        return pltpu.make_async_remote_copy(
            src_ref=src, dst_ref=dst, send_sem=send, recv_sem=recv, device_id={"chan": chan_to}, device_id_type=MESH
        )

    steps = range(1, side)
    moves = [(step, up) for step in range(side) for up in range(2)][1:]

    def to_group(seg, step):
        group, to = group_at(seg, step), peer(seg % 2, step)
        send, recv = first_send.at[seg, step - 1], first_recv.at[seg, step - 1]
        whole = remote(cand.at[seg, pl.ds(group * z.pair, z.pair)], recv_first.at[seg, step - 1], send, recv, to)
        single = remote(
            cand.at[seg, pl.ds(group * z.pair, 1)], recv_first.at[seg, step - 1, pl.ds(0, 1)], send, recv, to
        )
        return group < whole_groups, whole, single

    def to_slot(seg, n):
        step, up = moves[n]
        return kept(seg, step, up), remote(
            part.at[seg, slot_at(seg, step, up)], recv_second.at[seg, n], second_send.at[seg, n],
            second_recv.at[seg, n], peer(1 - seg % 2, step, up),
        )

    def tile_here(seg):
        return group_at(seg) * z.pair + slot_at(seg)

    def to_line(seg, n):
        return remote(
            mine.at[seg], full.at[seg, tile_here(seg)], line_send.at[seg, n], line_recv.at[seg, n],
            peer(1 - seg % 2, *moves[n]),
        )

    def to_all(seg, step):
        send, recv, to = group_send.at[seg, step - 1], group_recv.at[seg, step - 1], peer(seg % 2, step)
        whole = full.at[seg, pl.ds(group_at(seg) * z.pair, z.pair)]
        single = full.at[seg, pl.ds(group_at(seg) * z.pair, 1)]
        return remote(whole, whole, send, recv, to), remote(single, single, send, recv, to)

    def either(test, yes, no):
        pl.when(test)(yes)
        pl.when(jnp.logical_not(test))(no)

    def offer(seg):
        for step in steps:
            test, whole, single = to_group(seg, step)
            either(test, whole.start, single.start)

    def first(seg):
        def sum_tiles(count):
            for step in steps:
                to_group(seg, step)[1 if count > 1 else 2].wait_recv()
            for n in range(count):
                value = cand[seg, group_at(seg) * z.pair + n]
                for step in steps:
                    value = value + recv_first[seg, step - 1, n]
                part[seg, n] = value

        either(group_at(seg) < whole_groups, lambda: sum_tiles(z.pair), lambda: sum_tiles(1))
        for n in range(len(moves)):
            test, copy = to_slot(seg, n)
            pl.when(test)(copy.start)

    def second(seg):
        @pl.when(kept(seg))
        def _():
            for n in range(len(moves)):
                to_slot(seg, n)[1].wait_recv()
            value = part[seg, slot_at(seg)]
            for n in range(len(moves)):
                value = value + recv_second[seg, n]
            mine[seg] = value
            for n in range(len(moves)):
                to_line(seg, n).start()
            full[seg, tile_here(seg)] = value

    def forward(seg):
        for n, (step, up) in enumerate(moves):
            pl.when(kept(seg, side - step, up))(to_line(seg, n).wait_recv)
        for step in steps:
            whole, single = to_all(seg, step)
            either(group_at(seg) < whole_groups, whole.start, single.start)

    def arrive(seg):
        for step in steps:
            whole, single = to_all(seg, step)
            either(group_at(seg, side - step) < whole_groups, whole.wait_recv, single.wait_recv)

    def drain(seg):
        for step in steps:
            test, whole, single = to_group(seg, step)
            either(test, whole.wait_send, single.wait_send)
            whole, single = to_all(seg, step)
            either(group_at(seg) < whole_groups, whole.wait_send, single.wait_send)
        for n in range(len(moves)):
            test, copy = to_slot(seg, n)
            pl.when(test)(copy.wait_send)

        @pl.when(kept(seg))
        def _():
            for n in range(len(moves)):
                to_line(seg, n).wait_send()

    row = lax.broadcasted_iota(jnp.int32, (z.rows, z.channels), 0)
    wanted_row = jnp.zeros((z.rows, z.channels), jnp.int32)
    for n in range(z.rows):
        wanted_row = jnp.where(row == n, src_index[n // z.srcs, n % z.srcs], wanted_row)
    held = lax.broadcasted_iota(jnp.int32, (z.rows, z.channels), 1) + chan * z.channels
    onehot = (held == wanted_row).astype(jnp.float32).astype(jnp.bfloat16)

    def choose(seg):
        load(seg).wait()
        pick(z, records, seg, onehot, offsets[seg], cand)

    def power(seg):
        measure_power(z, records, seg, offsets[seg], factors)

    rows_a, rows_b = slice(0, FIRST_PART), slice(FIRST_PART, z.channels)

    def product(seg):
        arrive(seg)
        spread_lags(z, full, seg, turned)
        correlate(z, records, seg, rows_a, factors, turned, total)

    tasks = {"power": power, "first": first, "second": second, "forward": forward, "product": product}
    for name, seg in service_order(z):
        if name == "choose":
            choose(seg)
            if seg == 0:
                pl.semaphore_wait(barrier, peers)
            offer(seg)
        else:
            tasks[name](seg)

    def flip(rows, blocks):
        for at in range(rows.start, rows.stop, LANES):
            count, to = min(LANES, rows.stop - at), at - rows.start
            flipped[:, 0:count] = total[at : at + count, :].T
            for step in range(z.steps):
                for i in range(z.srcs):
                    value = flipped[pl.ds(step * z.srcs + i, LAGS, stride=z.rows), :]
                    blocks[step, i * LAGS : (i + 1) * LAGS, to : to + count] = value[:, 0:count]

    def send(src, dst, number, to):
        return pltpu.make_async_remote_copy(
            src_ref=src, dst_ref=dst, send_sem=win_send.at[number], recv_sem=win_recv.at[number],
            device_id={"win": to}, device_id_type=MESH,
        )

    def sum_over_win(number, blocks, pair_in, near_out, near_in):
        far = send(blocks.at[diagonal], pair_in.at[1], number, core_peer)
        own = send(blocks.at[core_peer], pair_in.at[0], number + 1, core_peer)
        last = send(near_out, near_in, number + 2, y_peer)

        def begin():
            far.start()
            own.start()

        def turn():
            far.wait_recv()
            near_out[...] = (blocks[y_peer] + pair_in[1]).astype(near_out.dtype)
            last.start()

        def end():
            own.wait_recv()
            last.wait_recv()
            return blocks[win] + pair_in[0] + near_in[...].astype(jnp.float32)

        return begin, turn, end, (far, own, last)

    begin_a, turn_a, end_a, copies_a = sum_over_win(0, blocks_a, pair_a, near_out_a, near_in_a)
    begin_b, turn_b, end_b, copies_b = sum_over_win(3, blocks_b, pair_b, near_out_b, near_in_b)
    flip(rows_a, blocks_a)
    begin_a()
    for seg in range(z.segs):
        if seg == z.segs // 2:
            turn_a()
        correlate(z, records, seg, rows_b, factors, turned, total)
    flip(rows_b, blocks_b)
    begin_b()
    for seg in range(z.segs):
        drain(seg)
    out[0, :, rows_a] = end_a()
    turn_b()
    out[0, :, rows_b] = end_b()
    for copy in copies_a + copies_b:
        copy.wait_send()


def body(chans, wins, records, offsets, src_index, quality):
    z = Sizes(*records.shape, offsets.shape[0], *src_index.shape, chans, wins)
    smem = pl.BlockSpec(memory_space=pltpu.SMEM)
    vmem = pl.BlockSpec(memory_space=pltpu.VMEM)
    hbm = pl.BlockSpec(memory_space=pl.ANY)
    bf16, f32 = jnp.bfloat16, jnp.float32
    dma = pltpu.SemaphoreType.DMA
    tile = (z.rows, LANES)
    block = (z.srcs * LAGS, z.channels)
    moves = 2 * z.side - 1
    shares = []
    for width in (FIRST_PART, z.channels - FIRST_PART):
        share = (block[0], width)
        shares += [pltpu.VMEM((z.steps, *share), f32), pltpu.VMEM((2, *share), f32)]
        shares += [pltpu.VMEM(share, bf16)] * 2
    sums = pl.pallas_call(
        functools.partial(main_kernel, z),
        out_shape=jax.ShapeDtypeStruct((1, *block), f32),
        in_specs=[smem, smem, hbm],
        out_specs=vmem,
        scratch_shapes=[
            pltpu.VMEM((z.segs, z.channels, z.width), bf16),
            pltpu.VMEM((z.segs, z.channels, LANES), f32),
            pltpu.VMEM((z.segs, z.slots, *tile), bf16),
            pltpu.VMEM((z.segs, z.side - 1, z.pair, *tile), bf16),
            pltpu.VMEM((z.segs, z.pair, *tile), bf16),
            pltpu.VMEM((z.segs, moves, *tile), bf16),
            pltpu.VMEM((z.segs, *tile), bf16),
            pltpu.VMEM((z.segs, z.slots, *tile), bf16),
            pltpu.VMEM((z.segs, z.zrows, LANES), bf16),
            pltpu.VMEM((z.channels, z.groups * LANES), f32),
            pltpu.VMEM((z.groups * LANES, LANES), f32),
            *shares,
            dma((z.segs,)),
            dma((z.segs, z.side - 1)),
            dma((z.segs, z.side - 1)),
            dma((z.segs, moves)),
            dma((z.segs, moves)),
            dma((z.segs, moves)),
            dma((z.segs, moves)),
            dma((z.segs, z.side - 1)),
            dma((z.segs, z.side - 1)),
            dma((6,)),
            dma((6,)),
        ],
        compiler_params=pltpu.CompilerParams(
            collective_id=0, has_side_effects=True, vmem_limit_bytes=VMEM_BYTES
        ),
        name="stack",
    )(src_index, offsets, records)
    scale = 1.0 / math.sqrt(z.segs * z.wins * L)
    return sums * scale * quality.astype(f32)[None, None, :]


def solution(mesh):
    return jax.shard_map(
        functools.partial(body, mesh.shape["chan"], mesh.shape["win"]),
        mesh=mesh,
        in_specs=(P("chan", "win"), P("win"), P(), P("chan")),
        out_specs=P("win", None, "chan"),
        check_vma=False,
    )
```
